512 devices in a mesh: member: 16 (over x, y_lo), lat: 32 (over z, y_hi, core).
Axes of the slice: x: 4, y: 8 (y_hi: 2, y_lo: 4; y = y_hi * 4 + y_lo), z: 8, core: 2. Of those that a mesh axis runs over, the one named last changes fastest.
Arguments:
- states: bfloat16 [16, 64, 256, 256], P('member', 'lat'), may hold values from -6 to 6
- member_id: int32 [16], P('member'), may hold values from 0 to 15, each once
- member_gain: float32 [16, 256], replicated, may hold values from 0.5 to 2
- first_conv: bfloat16 [2304, 256], P('member'), may hold values from -0.125 to 0.125
- second_conv: bfloat16 [2304, 256], P('member'), may hold values from -0.125 to 0.125
- head: bfloat16 [256, 8], replicated, may hold values from -0.375 to 0.375
- target: float32 [8, 64, 256], P(None, 'lat'), may hold values from -6 to 6
- lat_start: int32 [1], replicated, may hold values from 0 to 1737
Outputs:
- score: float32 [8, 64, 256], P(None, 'lat')
- mean_score: float32 [], replicated
The draws below stay inside these ranges and needn't reach their ends.
All inputs are finite; a program needn't handle non-finite values.
Results may differ from the reference program's by a relative error of at most 0.0018.
Values may be sent and summed in bfloat16 or wider, within the bound.
No kernel may reach another device: no remote copies, remote signals or barrier semaphores. Data moves between devices by JAX's collectives and lax.ppermute only.
A program may use at most 64 MiB of HBM per device.

```python
import math
import jax
import jax.numpy as jnp
from jax import lax

C = 256
K = 8
W = 256
M = 16
ROWS = 64


def levels(stream_key, dims, split, smallest, largest):
    loudness, own = 1.0, jax.random.fold_in(stream_key, 6)
    for dim, parts in split:
        draws = jnp.exp(jax.random.uniform(jax.random.fold_in(own, dim), (parts,), jnp.float32, smallest / len(split), largest / len(split)))
        loudness = loudness * jnp.repeat(draws, dims[dim] // parts).reshape([-1 if axis == dim else 1 for axis in range(len(dims))])
    return loudness


def scatter_about(rng, extent, width, limit, pieces=(), held_as=jnp.bfloat16):
    entries = width * jax.random.normal(rng, extent, jnp.float32)
    if pieces:
        entries = entries * levels(rng, extent, pieces, -0.22, 0.18)
    return jnp.clip(entries, -limit, limit).astype(held_as)


def setup_inputs(seed: int = 0) -> dict:
    key_list = jax.random.split(jax.random.key(seed), 9)
    return {
        "states": scatter_about(key_list[0], (M, ROWS, W, C), 1.0, 6.0, ((0, 16), (1, 32))),
        "member_id": jax.random.permutation(key_list[1], M).astype(jnp.int32),
        "member_gain": jnp.clip(jnp.exp(jax.random.uniform(key_list[2], (M, C), jnp.float32, math.log(0.5), math.log(2.0))), 0.5, 2.0),
        "first_conv": scatter_about(key_list[3], (9 * C, C), (9 * C) ** -0.5, 0.125, ((0, 16),)),
        "second_conv": scatter_about(key_list[4], (9 * C, C), (9 * C) ** -0.5, 0.125, ((0, 16),)),
        "head": scatter_about(key_list[5], (C, K), C ** -0.5, 0.375),
        "target": scatter_about(key_list[6], (K, ROWS, W), 1.0, 6.0, ((1, 32),), jnp.float32),
        "lat_start": jax.random.randint(key_list[7], (1,), 0, 1802 - ROWS).astype(jnp.int32),
    }


def product(left, right):
    return jnp.dot(left.astype(jnp.float32), right.astype(jnp.float32), precision=lax.Precision.HIGHEST, preferred_element_type=jnp.float32)


def convolve(field, weight):
    rows, cols, chans = field.shape
    padded = jnp.pad(field, ((1, 1), (1, 1), (0, 0)))
    taps = [padded[dy:dy + rows, dx:dx + cols, :] for dy in range(3) for dx in range(3)]
    patches = jnp.concatenate(taps, axis=-1).reshape(rows * cols, 9 * chans)
    return product(patches, weight).reshape(rows, cols, -1)


def reference(states, member_id, member_gain, first_conv, second_conv, head, target, lat_start):
    def one_member(args):
        state, ident = args
        select = (jnp.arange(M, dtype=jnp.int32) == ident).astype(jnp.float32)
        gain = jnp.dot(select, member_gain, precision=lax.Precision.HIGHEST)
        start = (state.astype(jnp.float32) * gain).astype(jnp.bfloat16)
        inner = jax.nn.gelu(convolve(start, first_conv), approximate=True).astype(jnp.bfloat16)
        block = (start.astype(jnp.float32) + convolve(inner, second_conv)).astype(jnp.bfloat16)
        pred = product(block.reshape(-1, C), head)
        return pred.T.reshape(K, ROWS, W).astype(jnp.bfloat16)

    preds = lax.map(one_member, (states, member_id)).astype(jnp.float32)
    skill = jnp.sum(jnp.abs(preds - target[None]), axis=0) / M

    def pair_step(total, index):
        return total + jnp.sum(jnp.abs(preds[index][None] - preds), axis=0), None

    spread, _ = lax.scan(pair_step, jnp.zeros((K, ROWS, W), jnp.float32), jnp.arange(M))
    eps = 0.05 / M
    score = skill - (1.0 - eps) / (2.0 * M * (M - 1)) * spread
    rows = lat_start[0].astype(jnp.float32) + jnp.arange(ROWS, dtype=jnp.float32)
    area = jnp.cos(jnp.pi * (90.0 - 0.1 * rows) / 180.0)
    mean_score = jnp.sum(score * area[None, :, None]) / (K * W * jnp.sum(area))
    return score, mean_score
```

```python
import functools

import jax
import jax.numpy as jnp
from jax import lax
from jax.experimental import pallas as pl
from jax.experimental.pallas import tpu as pltpu
from jax.sharding import PartitionSpec as P

MEMBERS, BANDS = 16, 32
AXES = ("member", "lat")


def partner_in_y(member, lat, flip):
    low, high = member % 4, lat // 2 % 2
    if flip == 1:
        return member ^ 1, lat
    return member ^ 3, lat ^ 2 if low in (0, 3) else lat


def partner_in_x(member, lat, flip):
    return member ^ (4 * flip), lat


def pairing(partner, step):
    pairs = []
    for member in range(MEMBERS):
        for lat in range(BANDS):
            flip = (1, 3)[(lat + step) % 2]
            other = partner(member, lat, flip)
            pairs.append((member * BANDS + lat, other[0] * BANDS + other[1]))
    return pairs


def swap(block, partner, step):
    return lax.ppermute(block, AXES, pairing(partner, step))


def tap_sum(shifted, weights, first, rows):
    cols, chans = shifted.shape[2], shifted.shape[3]
    total = None
    for dy in range(3):
        for dx in range(3):
            left = shifted[dx, first + dy : first + dy + rows].reshape(rows * cols, chans)
            base = (dy * 3 + dx) * chans
            right = jnp.concatenate(
                [weights[0, base : base + chans], weights[1, base : base + chans]], axis=1
            )
            term = jnp.dot(left, right, preferred_element_type=jnp.float32)
            total = term if total is None else total + term
    return total


def put_shifted(shifted, row, value):
    cols = value.shape[0]
    column = lax.broadcasted_iota(jnp.int32, value.shape, 0)
    before = jnp.where(column == 0, 0.0, pltpu.roll(value, 1, 0))
    after = jnp.where(column == cols - 1, 0.0, pltpu.roll(value, cols - 1, 0))
    shifted[0, row] = before.astype(jnp.bfloat16)
    shifted[1, row] = value.astype(jnp.bfloat16)
    shifted[2, row] = after.astype(jnp.bfloat16)


def put_weights(weights, core, member, blocks, depth):
    turns = jnp.where(core == 0, 1, 3)
    masks = (0, turns, turns ^ 2, 2)
    at = 0
    for ref in blocks:
        for index in range(ref.shape[0]):
            mask = masks[at // 4] * 4 + masks[at % 4]
            origin = (member ^ mask) * depth
            weights[core, pl.ds(pl.multiple_of(origin, 16), depth), :] = ref[index]
            at += 1


def first_kernel(
    ident, gains, own, near, far, mine_a, mine_b, other_a, other_b, inner, shifted, weights
):
    member, lat = lax.axis_index("member"), lax.axis_index("lat")
    core = lat % 2
    depth = mine_a.shape[1]
    gain = gains[pl.ds(ident[0], 1), :]
    rows = own.shape[0]
    for ref, base in ((own, rows), (near, 2 * rows * (1 - core)), (far, 2 * rows * core)):
        for row in range(rows):
            value = (ref[row].astype(jnp.float32) * gain).astype(jnp.bfloat16)
            put_shifted(shifted, base + row, value.astype(jnp.float32))
    put_weights(weights, core, member, (mine_a, mine_b), depth)
    put_weights(weights, 1 - core, member, (other_a, other_b), depth)
    for half in range(2):
        out = tap_sum(shifted, weights, 2 * half, 2)
        out = jax.nn.gelu(out, approximate=True)
        out = out.reshape(2, out.shape[0] // 2, out.shape[1])
        for row in range(2):
            value = out[row]
            if half == 0 and row == 0:
                value = jnp.where(lat == 0, 0.0, value)
            if half == 1 and row == 1:
                value = jnp.where(lat == BANDS - 1, 0.0, value)
            inner[2 * half + row] = value.astype(jnp.bfloat16)


def second_kernel(
    ident, gains, own, inner, head, mine_a, mine_b, other_a, other_b, pred, shifted, weights
):
    member, lat = lax.axis_index("member"), lax.axis_index("lat")
    core = lat % 2
    depth = mine_a.shape[1]
    gain = gains[pl.ds(ident[0], 1), :]
    for row in range(inner.shape[0]):
        put_shifted(shifted, row, inner[row].astype(jnp.float32))
    put_weights(weights, core, member, (mine_a, mine_b), depth)
    put_weights(weights, 1 - core, member, (other_a, other_b), depth)
    rows, cols, chans = own.shape
    out = tap_sum(shifted, weights, 0, rows)
    start = (own[...].reshape(rows * cols, chans).astype(jnp.float32) * gain).astype(jnp.bfloat16)
    block = (start.astype(jnp.float32) + out).astype(jnp.bfloat16)
    value = lax.dot_general(
        head[...], block, (((1,), (1,)), ((), ())), preferred_element_type=jnp.float32
    ).astype(jnp.bfloat16)
    for index in range(pred.shape[0]):
        pred[index] = value


def score_kernel(weight, fields, target, score, partial, *, factor):
    members = fields.shape[0]
    cols = target.shape[2]
    parts = []
    for row in range(target.shape[1]):
        span = slice(row * cols, (row + 1) * cols)
        values = [fields[m, :, span].astype(jnp.float32) for m in range(members)]
        truth = target[:, row, :]
        skill = functools.reduce(jnp.add, [jnp.abs(v - truth) for v in values])
        spread = functools.reduce(
            jnp.add,
            [
                functools.reduce(jnp.add, [jnp.abs(values[m] - values[n]) for n in range(m)])
                for m in range(1, members)
            ],
        )
        result = skill / members - (2.0 * factor) * spread
        score[:, row, :] = result
        parts.append(jnp.sum(result) * weight[row])
    partial[...] = jnp.full(partial.shape, functools.reduce(jnp.add, parts), jnp.float32)


VMEM = pl.BlockSpec(memory_space=pltpu.VMEM)
SMEM = pl.BlockSpec(memory_space=pltpu.SMEM)


def body(states, member_id, member_gain, first_conv, second_conv, head, target, lat_start):
    rows, cols, chans = (states.shape[1], states.shape[2], states.shape[3])
    depth = first_conv.shape[0]
    lat = lax.axis_index("lat")
    core = lat % 2
    own = states[0]

    half = chans // 2
    shard = jnp.stack([first_conv, second_conv])
    mine = jnp.where(core == 0, shard[:, :, :half], shard[:, :, half:])[None]
    mine = jnp.concatenate([mine, swap(mine, partner_in_y, 0)], axis=0)
    mine = jnp.concatenate([mine, swap(mine, partner_in_y, 1)], axis=0)
    mine = jnp.concatenate([mine, swap(mine, partner_in_x, 0)], axis=0)
    first_a, second_a = mine[:, 0], mine[:, 1]
    first_b = swap(first_a, partner_in_x, 1)
    second_b = swap(second_a, partner_in_x, 1)

    on_chip = [(lat_id, lat_id ^ 1) for lat_id in range(BANDS)]
    across = [(lat_id, ((lat_id + 1) ^ 1) - 1) for lat_id in range(1, BANDS - 1)]
    near = lax.ppermute(own, "lat", on_chip)
    far = lax.ppermute(own, "lat", across)
    others = [lax.ppermute(block, "lat", on_chip) for block in (first_a, first_b, second_a, second_b)]

    inner = pl.pallas_call(
        first_kernel,
        out_shape=jax.ShapeDtypeStruct((rows + 2, cols, chans), jnp.bfloat16),
        in_specs=[SMEM] + [VMEM] * 8,
        out_specs=VMEM,
        scratch_shapes=[
            pltpu.VMEM((3, 3 * rows, cols, chans), jnp.bfloat16),
            pltpu.VMEM((2, 9 * chans, half), jnp.bfloat16),
        ],
        cost_estimate=pl.CostEstimate(
            flops=2 * (rows + 2) * cols * 9 * chans * chans, bytes_accessed=4 << 20, transcendentals=0
        ),
        name="first",
    )(member_id, member_gain, own, near, far, first_a, first_b, others[0], others[1])
    pred = pl.pallas_call(
        second_kernel,
        out_shape=jax.ShapeDtypeStruct((MEMBERS, head.shape[1], rows * cols), jnp.bfloat16),
        in_specs=[SMEM] + [VMEM] * 8,
        out_specs=VMEM,
        scratch_shapes=[
            pltpu.VMEM((3, rows + 2, cols, chans), jnp.bfloat16),
            pltpu.VMEM((2, 9 * chans, half), jnp.bfloat16),
        ],
        cost_estimate=pl.CostEstimate(
            flops=2 * rows * cols * 9 * chans * chans, bytes_accessed=3 << 20, transcendentals=0
        ),
        name="second",
    )(member_id, member_gain, own, inner, head.T, second_a, second_b, others[2], others[3])
    fields = lax.all_to_all(pred, "member", 0, 0, tiled=True)

    row_ids = lat_start[0] + jnp.arange(BANDS * rows, dtype=jnp.int32)
    area = jnp.cos(jnp.pi * (90.0 - 0.1 * row_ids.astype(jnp.float32)) / 180.0)
    weight = lax.dynamic_slice(area, (lat * rows,), (rows,)) / (
        head.shape[1] * cols * jnp.sum(area)
    )
    eps = 0.05 / MEMBERS
    factor = (1.0 - eps) / (2.0 * MEMBERS * (MEMBERS - 1))
    score, partial = pl.pallas_call(
        functools.partial(score_kernel, factor=factor),
        out_shape=(
            jax.ShapeDtypeStruct(target.shape, jnp.float32),
            jax.ShapeDtypeStruct((BANDS, 1, 128), jnp.float32),
        ),
        in_specs=[SMEM, VMEM, VMEM],
        out_specs=(VMEM, VMEM),
        name="score",
    )(weight, fields, target)
    shares = lax.all_to_all(partial, "lat", 0, 0, tiled=True)
    return (score, jnp.sum(shares[:, 0, 0]))


def solution(mesh):
    assert mesh.shape["member"] == MEMBERS and mesh.shape["lat"] == BANDS
    placed = (
        P("member", "lat", None, None),
        P("member"),
        P(),
        P("member", None),
        P("member", None),
        P(),
        P(None, "lat", None),
        P(),
    )
    return jax.shard_map(
        body, mesh=mesh, in_specs=placed, out_specs=(P(None, "lat", None), P()), check_vma=False
    )
```

```python
import functools

import jax
import jax.numpy as jnp
from jax import lax
from jax.experimental import pallas as pl
from jax.experimental.pallas import tpu as pltpu
from jax.sharding import PartitionSpec as P

MEMBERS, BANDS = 16, 32
AXES = ("member", "lat")
LIMIT = 20 << 20


def partner_in_y(member, lat, flip):
    low = member % 4
    if flip == 1:
        return member ^ 1, lat
    return member ^ 3, lat ^ 2 if low in (0, 3) else lat


def partner_in_x(member, lat, flip):
    return member ^ (4 * flip), lat


def pairing(partner, step):
    pairs = []
    for member in range(MEMBERS):
        for lat in range(BANDS):
            flip = (1, 3)[(lat + step) % 2]
            other = partner(member, lat, flip)
            pairs.append((member * BANDS + lat, other[0] * BANDS + other[1]))
    return pairs


def swap(block, partner, step):
    return lax.ppermute(block, AXES, pairing(partner, step))


def mean_groups():
    groups = []
    for member in range(MEMBERS):
        groups.append(
            [(member ^ 2 * (lat // 2 % 2)) * BANDS + lat for lat in range(BANDS)]
        )
    return groups


def tap_sum(shifted, weights, first, rows):
    cols, chans = shifted.shape[2], shifted.shape[3]
    total = None
    for dy in range(3):
        for dx in range(3):
            left = shifted[dx, first + dy : first + dy + rows].reshape(rows * cols, chans)
            base = (dy * 3 + dx) * chans
            right = jnp.concatenate(
                [weights[0, base : base + chans], weights[1, base : base + chans]], axis=1
            )
            term = jnp.dot(left, right, preferred_element_type=jnp.float32)
            total = term if total is None else total + term
    return total


def put_shifted(shifted, row, value):
    cols = value.shape[0]
    column = lax.broadcasted_iota(jnp.int32, value.shape, 0)
    before = jnp.where(column == 0, 0.0, pltpu.roll(value, 1, 0))
    after = jnp.where(column == cols - 1, 0.0, pltpu.roll(value, cols - 1, 0))
    shifted[0, row] = before.astype(jnp.bfloat16)
    shifted[1, row] = value.astype(jnp.bfloat16)
    shifted[2, row] = after.astype(jnp.bfloat16)


def put_weights(weights, core, member, blocks, which):
    depth = blocks[0].shape[2]
    turns = jnp.where(core == 0, 1, 3)
    masks = (0, turns, turns ^ 2, 2)
    at = 0
    for ref in blocks:
        for index in range(ref.shape[0]):
            mask = masks[at // 4] * 4 + masks[at % 4]
            origin = (member ^ mask) * depth
            block = ref[index] if len(ref.shape) == 3 else ref[index, which]
            weights[core, pl.ds(pl.multiple_of(origin, 16), depth), :] = block
            at += 1


def first_kernel(
    ident, gains, own, near, far, mine_a, mine_b, other_a, other_b, inner, shifted, weights
):
    member, lat = lax.axis_index("member"), lax.axis_index("lat")
    core = lat % 2
    gain = gains[pl.ds(ident[0], 1), :]
    rows = own.shape[0]
    for ref, base in ((own, rows), (near, 2 * rows * (1 - core)), (far, 2 * rows * core)):
        for row in range(rows):
            value = (ref[row].astype(jnp.float32) * gain).astype(jnp.bfloat16)
            put_shifted(shifted, base + row, value.astype(jnp.float32))
    put_weights(weights, core, member, (mine_a, mine_b), 0)
    put_weights(weights, 1 - core, member, (other_a, other_b), 0)
    for half in range(2):
        out = tap_sum(shifted, weights, 2 * half, 2)
        out = jax.nn.gelu(out, approximate=True)
        out = out.reshape(2, out.shape[0] // 2, out.shape[1])
        for row in range(2):
            value = out[row]
            if half == 0 and row == 0:
                value = jnp.where(lat == 0, 0.0, value)
            if half == 1 and row == 1:
                value = jnp.where(lat == BANDS - 1, 0.0, value)
            inner[2 * half + row] = value.astype(jnp.bfloat16)


def second_kernel(
    ident, gains, own, inner, head, mine_a, mine_b, other_a, other_b, pred, shifted, weights
):
    member, lat = lax.axis_index("member"), lax.axis_index("lat")
    core = lat % 2
    gain = gains[pl.ds(ident[0], 1), :]
    for row in range(inner.shape[0]):
        put_shifted(shifted, row, inner[row].astype(jnp.float32))
    put_weights(weights, core, member, (mine_a, mine_b), 1)
    put_weights(weights, 1 - core, member, (other_a, other_b), 1)
    rows, cols, chans = own.shape
    out = tap_sum(shifted, weights, 0, rows)
    start = (own[...].reshape(rows * cols, chans).astype(jnp.float32) * gain).astype(jnp.bfloat16)
    block = (start.astype(jnp.float32) + out).astype(jnp.bfloat16)
    value = lax.dot_general(
        head[...], block, (((1,), (1,)), ((), ())), preferred_element_type=jnp.float32
    ).astype(jnp.bfloat16)
    for index in range(pred.shape[0]):
        pred[index] = value


def score_kernel(weight, fields, target, score, partial, *, factor):
    members = fields.shape[0]
    cols = target.shape[2]
    parts = []
    for row in range(target.shape[1]):
        span = slice(row * cols, (row + 1) * cols)
        values = [fields[m, :, span].astype(jnp.float32) for m in range(members)]
        truth = target[:, row, :]
        skill = functools.reduce(jnp.add, [jnp.abs(v - truth) for v in values])
        spread = functools.reduce(
            jnp.add,
            [
                functools.reduce(jnp.add, [jnp.abs(values[m] - values[n]) for n in range(m)])
                for m in range(1, members)
            ],
        )
        result = skill / members - (2.0 * factor) * spread
        score[:, row, :] = result
        parts.append(jnp.sum(result) * weight[row])
    partial[...] = jnp.full(partial.shape, functools.reduce(jnp.add, parts), jnp.float32)


VMEM = pl.BlockSpec(memory_space=pltpu.VMEM)
SMEM = pl.BlockSpec(memory_space=pltpu.SMEM)


def body(states, member_id, member_gain, first_conv, second_conv, head, target, lat_start):
    rows, cols, chans = (states.shape[1], states.shape[2], states.shape[3])
    lat = lax.axis_index("lat")
    core = lat % 2
    own = states[0]

    half = chans // 2
    shard = jnp.stack([first_conv, second_conv])
    mine = jnp.where(core == 0, shard[:, :, :half], shard[:, :, half:])[None]
    mine = jnp.concatenate([mine, swap(mine, partner_in_y, 0)], axis=0)
    mine = jnp.concatenate([mine, swap(mine, partner_in_y, 1)], axis=0)
    mine = jnp.concatenate([mine, swap(mine, partner_in_x, 0)], axis=0)
    first_a, second_a = mine[:, 0], mine[:, 1]
    first_b = swap(first_a, partner_in_x, 1)
    second_b = swap(second_a, partner_in_x, 1)

    on_chip = [(lat_id, lat_id ^ 1) for lat_id in range(BANDS)]
    across = [(lat_id, ((lat_id + 1) ^ 1) - 1) for lat_id in range(1, BANDS - 1)]
    near = lax.ppermute(own, "lat", on_chip)
    far = lax.ppermute(own, "lat", across)
    other = lax.ppermute(mine, "lat", on_chip)
    first_o = lax.ppermute(first_b, "lat", on_chip)
    second_o = lax.ppermute(second_b, "lat", on_chip)

    inner = pl.pallas_call(
        first_kernel,
        out_shape=jax.ShapeDtypeStruct((rows + 2, cols, chans), jnp.bfloat16),
        in_specs=[SMEM] + [VMEM] * 8,
        out_specs=VMEM,
        scratch_shapes=[
            pltpu.VMEM((3, 3 * rows, cols, chans), jnp.bfloat16),
            pltpu.VMEM((2, 9 * chans, half), jnp.bfloat16),
        ],
        cost_estimate=pl.CostEstimate(
            flops=2 * (rows + 2) * cols * 9 * chans * chans, bytes_accessed=4 << 20, transcendentals=0
        ),
        compiler_params=pltpu.CompilerParams(vmem_limit_bytes=LIMIT),
        name="first",
    )(member_id, member_gain, own, near, far, mine, first_b, other, first_o)
    pred = pl.pallas_call(
        second_kernel,
        out_shape=jax.ShapeDtypeStruct((MEMBERS, head.shape[1], rows * cols), jnp.bfloat16),
        in_specs=[SMEM] + [VMEM] * 8,
        out_specs=VMEM,
        scratch_shapes=[
            pltpu.VMEM((3, rows + 2, cols, chans), jnp.bfloat16),
            pltpu.VMEM((2, 9 * chans, half), jnp.bfloat16),
        ],
        cost_estimate=pl.CostEstimate(
            flops=2 * rows * cols * 9 * chans * chans, bytes_accessed=3 << 20, transcendentals=0
        ),
        compiler_params=pltpu.CompilerParams(vmem_limit_bytes=LIMIT),
        name="second",
    )(member_id, member_gain, own, inner, head.T, mine, second_b, other, second_o)
    fields = lax.all_to_all(pred, "member", 0, 0, tiled=True)

    row_ids = lat_start[0] + jnp.arange(BANDS * rows, dtype=jnp.int32)
    area = jnp.cos(jnp.pi * (90.0 - 0.1 * row_ids.astype(jnp.float32)) / 180.0)
    weight = lax.dynamic_slice(area, (lat * rows,), (rows,)) / (
        head.shape[1] * cols * jnp.sum(area)
    )
    eps = 0.05 / MEMBERS
    factor = (1.0 - eps) / (2.0 * MEMBERS * (MEMBERS - 1))
    score, partial = pl.pallas_call(
        functools.partial(score_kernel, factor=factor),
        out_shape=(
            jax.ShapeDtypeStruct(target.shape, jnp.float32),
            jax.ShapeDtypeStruct((BANDS, 1, 128), jnp.float32),
        ),
        in_specs=[SMEM, VMEM, VMEM],
        out_specs=(VMEM, VMEM),
        compiler_params=pltpu.CompilerParams(vmem_limit_bytes=LIMIT),
        name="score",
    )(weight, fields, target)
    shares = lax.all_to_all(
        partial, AXES, 0, 0, axis_index_groups=mean_groups(), tiled=True
    )
    return (score, jnp.sum(shares[:, 0, 0]))


def solution(mesh):
    assert mesh.shape["member"] == MEMBERS and mesh.shape["lat"] == BANDS
    placed = (
        P("member", "lat", None, None),
        P("member"),
        P(),
        P("member", None),
        P("member", None),
        P(),
        P(None, "lat", None),
        P(),
    )

    return jax.shard_map(
        body, mesh=mesh, in_specs=placed, out_specs=(P(None, "lat", None), P()), check_vma=False
    )
```

```python
import functools

import jax
import jax.numpy as jnp
from jax import lax
from jax.experimental import pallas as pl
from jax.experimental.pallas import tpu as pltpu
from jax.sharding import PartitionSpec as P

MEMBERS, BANDS = 16, 32
AXES = ("member", "lat")
LIMIT = 20 << 20


def partner_in_y(member, lat, flip):
    low = member % 4
    if flip == 1:
        return member ^ 1, lat
    return member ^ 3, lat ^ 2 if low in (0, 3) else lat


def partner_in_x(member, lat, flip):
    return member ^ (4 * flip), lat


def pairing(partner, step):
    pairs = []
    for member in range(MEMBERS):
        for lat in range(BANDS):
            flip = (1, 3)[(lat + step) % 2]
            other = partner(member, lat, flip)
            pairs.append((member * BANDS + lat, other[0] * BANDS + other[1]))
    return pairs


def swap(block, partner, step):
    return lax.ppermute(block, AXES, pairing(partner, step))


def far_relays():
    there, onward = [], []
    for member in range(MEMBERS):
        for lat in range(BANDS):
            step = 1 if lat % 2 else -1
            y = (lat // 2 % 2 * 4 + member % 4 + 2 * step) % 8
            middle = (member // 4 * 4 + y % 4) * BANDS + lat // 4 * 4 + y // 4 * 2 + lat % 2
            there.append((member * BANDS + lat, middle))
            if 0 <= lat + step < BANDS:
                onward.append((middle, member * BANDS + lat + step))
    return there, onward


def mean_groups():
    groups = []
    for member in range(MEMBERS):
        groups.append(
            [(member ^ 2 * (lat // 2 % 2)) * BANDS + lat for lat in range(BANDS)]
        )
    return groups


def tap_sum(shifted, weights, first, rows):
    cols, chans = shifted.shape[2], shifted.shape[3]
    total = None
    for dy in range(3):
        for dx in range(3):
            left = shifted[dx, first + dy : first + dy + rows].reshape(rows * cols, chans)
            base = (dy * 3 + dx) * chans
            right = jnp.concatenate(
                [weights[0, base : base + chans], weights[1, base : base + chans]], axis=1
            )
            term = jnp.dot(left, right, preferred_element_type=jnp.float32)
            total = term if total is None else total + term
    return total


def put_shifted(shifted, row, value):
    cols = value.shape[0]
    column = lax.broadcasted_iota(jnp.int32, value.shape, 0)
    before = jnp.where(column == 0, 0.0, pltpu.roll(value, 1, 0))
    after = jnp.where(column == cols - 1, 0.0, pltpu.roll(value, cols - 1, 0))
    shifted[0, row] = before.astype(jnp.bfloat16)
    shifted[1, row] = value.astype(jnp.bfloat16)
    shifted[2, row] = after.astype(jnp.bfloat16)


def put_weights(weights, core, member, blocks, which):
    depth = blocks[0].shape[2]
    turns = jnp.where(core == 0, 1, 3)
    masks = (0, turns, turns ^ 2, 2)
    at = 0
    for ref in blocks:
        for index in range(ref.shape[-3]):
            mask = masks[at // 4] * 4 + masks[at % 4]
            origin = (member ^ mask) * depth
            block = ref[index] if len(ref.shape) == 3 else ref[which, index]
            weights[core, pl.ds(pl.multiple_of(origin, 16), depth), :] = block
            at += 1


def first_kernel(
    ident, gains, own, near, far, mine_a, mine_b, other_a, other_b, inner, shifted, weights
):
    member, lat = lax.axis_index("member"), lax.axis_index("lat")
    core = lat % 2
    gain = gains[pl.ds(ident[0], 1), :]
    rows = own.shape[0]
    for ref, base in ((own, rows), (near, 2 * rows * (1 - core)), (far, 2 * rows * core)):
        for row in range(rows):
            value = (ref[row].astype(jnp.float32) * gain).astype(jnp.bfloat16)
            put_shifted(shifted, base + row, value.astype(jnp.float32))
    put_weights(weights, core, member, (mine_a, mine_b), 0)
    put_weights(weights, 1 - core, member, (other_a, other_b), 0)
    for half in range(2):
        out = tap_sum(shifted, weights, 2 * half, 2)
        out = jax.nn.gelu(out, approximate=True)
        out = out.reshape(2, out.shape[0] // 2, out.shape[1])
        for row in range(2):
            value = out[row]
            if half == 0 and row == 0:
                value = jnp.where(lat == 0, 0.0, value)
            if half == 1 and row == 1:
                value = jnp.where(lat == BANDS - 1, 0.0, value)
            inner[2 * half + row] = value.astype(jnp.bfloat16)


def second_kernel(
    ident, gains, own, inner, head, mine_a, mine_b, other_a, other_b, pred, shifted, weights
):
    member, lat = lax.axis_index("member"), lax.axis_index("lat")
    core = lat % 2
    gain = gains[pl.ds(ident[0], 1), :]
    for row in range(inner.shape[0]):
        put_shifted(shifted, row, inner[row].astype(jnp.float32))
    put_weights(weights, core, member, (mine_a, mine_b), 1)
    put_weights(weights, 1 - core, member, (other_a, other_b), 1)
    rows, cols, chans = own.shape
    out = tap_sum(shifted, weights, 0, rows)
    start = (own[...].reshape(rows * cols, chans).astype(jnp.float32) * gain).astype(jnp.bfloat16)
    block = (start.astype(jnp.float32) + out).astype(jnp.bfloat16)
    value = lax.dot_general(
        head[...], block, (((1,), (1,)), ((), ())), preferred_element_type=jnp.float32
    ).astype(jnp.bfloat16)
    for index in range(pred.shape[0]):
        pred[index] = value


def score_kernel(weight, fields, target, score, partial, *, factor):
    members = fields.shape[0]
    cols = target.shape[2]
    parts = []
    for row in range(target.shape[1]):
        span = slice(row * cols, (row + 1) * cols)
        values = [fields[m, :, span].astype(jnp.float32) for m in range(members)]
        truth = target[:, row, :]
        skill = functools.reduce(jnp.add, [jnp.abs(v - truth) for v in values])
        spread = functools.reduce(
            jnp.add,
            [
                functools.reduce(jnp.add, [jnp.abs(values[m] - values[n]) for n in range(m)])
                for m in range(1, members)
            ],
        )
        result = skill / members - (2.0 * factor) * spread
        score[:, row, :] = result
        parts.append(jnp.sum(result) * weight[row])
    partial[...] = jnp.full(partial.shape, functools.reduce(jnp.add, parts), jnp.float32)


VMEM = pl.BlockSpec(memory_space=pltpu.VMEM)
SMEM = pl.BlockSpec(memory_space=pltpu.SMEM)


def body(states, member_id, member_gain, first_conv, second_conv, head, target, lat_start):
    rows, cols, chans = (states.shape[1], states.shape[2], states.shape[3])
    lat = lax.axis_index("lat")
    core = lat % 2
    own = states[0]

    half = chans // 2
    shard = jnp.stack([first_conv, second_conv])
    mine = jnp.where(core == 0, shard[:, :, :half], shard[:, :, half:])[:, None]
    mine = jnp.concatenate([mine, swap(mine, partner_in_y, 0)], axis=1)
    mine = jnp.concatenate([mine, swap(mine, partner_in_y, 1)], axis=1)
    mine = jnp.concatenate([mine, swap(mine, partner_in_x, 0)], axis=1)
    first_a, second_a = mine[0], mine[1]
    first_b = swap(first_a, partner_in_x, 1)
    second_b = swap(second_a, partner_in_x, 1)

    on_chip = [(lat_id, lat_id ^ 1) for lat_id in range(BANDS)]
    near = lax.ppermute(own, "lat", on_chip)
    there, onward = far_relays()
    far = lax.ppermute(own, AXES, there)
    far = lax.ppermute(far, AXES, onward)
    other = lax.ppermute(mine, "lat", on_chip)
    first_o = lax.ppermute(first_b, "lat", on_chip)
    second_o = lax.ppermute(second_b, "lat", on_chip)

    inner = pl.pallas_call(
        first_kernel,
        out_shape=jax.ShapeDtypeStruct((rows + 2, cols, chans), jnp.bfloat16),
        in_specs=[SMEM] + [VMEM] * 8,
        out_specs=VMEM,
        scratch_shapes=[
            pltpu.VMEM((3, 3 * rows, cols, chans), jnp.bfloat16),
            pltpu.VMEM((2, 9 * chans, half), jnp.bfloat16),
        ],
        cost_estimate=pl.CostEstimate(
            flops=2 * (rows + 2) * cols * 9 * chans * chans, bytes_accessed=4 << 20, transcendentals=0
        ),
        compiler_params=pltpu.CompilerParams(vmem_limit_bytes=LIMIT),
        name="first",
    )(member_id, member_gain, own, near, far, mine, first_b, other, first_o)
    pred = pl.pallas_call(
        second_kernel,
        out_shape=jax.ShapeDtypeStruct((MEMBERS, head.shape[1], rows * cols), jnp.bfloat16),
        in_specs=[SMEM] + [VMEM] * 8,
        out_specs=VMEM,
        scratch_shapes=[
            pltpu.VMEM((3, rows + 2, cols, chans), jnp.bfloat16),
            pltpu.VMEM((2, 9 * chans, half), jnp.bfloat16),
        ],
        cost_estimate=pl.CostEstimate(
            flops=2 * rows * cols * 9 * chans * chans, bytes_accessed=3 << 20, transcendentals=0
        ),
        compiler_params=pltpu.CompilerParams(vmem_limit_bytes=LIMIT),
        name="second",
    )(member_id, member_gain, own, inner, head.T, mine, second_b, other, second_o)
    fields = lax.all_to_all(pred, "member", 0, 0, tiled=True)

    row_ids = lat_start[0] + jnp.arange(BANDS * rows, dtype=jnp.int32)
    area = jnp.cos(jnp.pi * (90.0 - 0.1 * row_ids.astype(jnp.float32)) / 180.0)
    weight = lax.dynamic_slice(area, (lat * rows,), (rows,)) / (
        head.shape[1] * cols * jnp.sum(area)
    )
    eps = 0.05 / MEMBERS
    factor = (1.0 - eps) / (2.0 * MEMBERS * (MEMBERS - 1))
    score, partial = pl.pallas_call(
        functools.partial(score_kernel, factor=factor),
        out_shape=(
            jax.ShapeDtypeStruct(target.shape, jnp.float32),
            jax.ShapeDtypeStruct((BANDS, 1, 128), jnp.float32),
        ),
        in_specs=[SMEM, VMEM, VMEM],
        out_specs=(VMEM, VMEM),
        compiler_params=pltpu.CompilerParams(vmem_limit_bytes=LIMIT),
        name="score",
    )(weight, fields, target)
    shares = lax.all_to_all(
        partial, AXES, 0, 0, axis_index_groups=mean_groups(), tiled=True
    )
    return (score, jnp.sum(shares[:, 0, 0]))


def solution(mesh):
    assert mesh.shape["member"] == MEMBERS and mesh.shape["lat"] == BANDS
    placed = (
        P("member", "lat", None, None),
        P("member"),
        P(),
        P("member", None),
        P("member", None),
        P(),
        P(None, "lat", None),
        P(),
    )

    return jax.shard_map(
        body, mesh=mesh, in_specs=placed, out_specs=(P(None, "lat", None), P()), check_vma=False
    )
```
